512 devices in a mesh: mem: 32 (over x, y_lo, core), tile: 16 (over z, y_hi).
Axes of the slice: x: 4, y: 8 (y_hi: 2, y_lo: 4; y = y_hi * 4 + y_lo), z: 8, core: 2. Of those that a mesh axis runs over, the one named last changes fastest.
Arguments:
- background: float32 [256, 2048, 256], P('mem', 'tile'), may hold values from -6 to 6
- diffusion: float32 [256], replicated, may hold values from 0.05 to 0.2
- advection: float32 [256], replicated, may hold values from -0.25 to 0.25
- obs_where: int32 [16, 128, 512], P('tile'), may hold values from 0 to 255
- obs_count: int32 [16, 128], P('tile'), may hold values from 256 to 512
- obs_value: float32 [16, 128, 512], P('tile'), may hold values from -6 to 6
- obs_rinv: float32 [16, 128, 512], P('tile'), may hold values from 1 to 1000
Outputs:
- analysis: float32 [256, 2048, 256], P('mem', 'tile')
The draws below stay inside these ranges and needn't reach their ends.
Inputs may be any that keep to these rules, and one draw needn't show every extreme that they name: `obs_where`: each slot reads one entry of its column's 4 * 64 state entries. A column uses its first obs_count slots.
All inputs are finite; a program needn't handle non-finite values.
Results may differ from the reference program's by a relative error of at most 0.0003.
Values sent between devices are 32-bit elements; how exact they have to be, the bound alone decides.
A program may use at most 64 MiB of HBM per device.

```python
import math
import jax
import jax.numpy as jnp
from jax import lax

MEMBERS = 256
LEVELS = 64
VARS = 4
OBS_MAX = 512
ITERS = 12
COLS_TILE = 128
TILES = 16
COLS = 2048


def plant(values, stream_key, smallest, high):
    extent = values.shape
    index_at = [jax.random.randint(jax.random.fold_in(stream_key, axis), (), 0, extent[axis]) for axis in range(len(extent))]
    values = values.at[tuple(index_at)].set(smallest)
    longest = extent.index(max(extent))
    index_at[longest] = (index_at[longest] + 1) % extent[longest]
    return values.at[tuple(index_at)].set(high)


def block_levels(rng, shape, cuts, least, top_value):
    gain, own = 1.0, jax.random.fold_in(rng, 6)
    for position, shards_of in cuts:
        steps = jnp.exp(jax.random.uniform(jax.random.fold_in(own, position), (shards_of,), jnp.float32, least / len(cuts), top_value / len(cuts)))
        gain = gain * jnp.repeat(steps, shape[position] // shards_of).reshape([-1 if axis == position else 1 for axis in range(len(shape))])
    return gain


def scatter_about(rng, extent, spread, bound, shards=(), kind=jnp.bfloat16):
    array = spread * jax.random.normal(rng, extent, jnp.float32)
    if shards:
        array = array * block_levels(rng, extent, shards, -0.22, 0.18)
    return jnp.clip(array, -bound, bound).astype(kind)


def setup_inputs(seed: int = 0) -> dict:
    keys = jax.random.split(jax.random.key(seed), 8)
    background = scatter_about(keys[0], (MEMBERS, COLS, VARS * LEVELS), 1.0, 6.0, ((0, 32), (1, 16)), jnp.float32)
    diffusion = jnp.clip(jax.random.uniform(keys[1], (VARS * LEVELS,), jnp.float32, 0.05, 0.2), 0.05, 0.2)
    advection = jnp.clip(jax.random.uniform(keys[2], (VARS * LEVELS,), jnp.float32, -0.25, 0.25), -0.25, 0.25)
    obs_where = plant(jax.random.randint(keys[3], (TILES, COLS_TILE, OBS_MAX), 0, VARS * LEVELS), jax.random.fold_in(keys[3], 1), 0, (VARS * LEVELS) - 1).astype(jnp.int32)
    obs_count = plant(jax.random.randint(keys[4], (TILES, COLS_TILE), OBS_MAX // 2, OBS_MAX + 1), jax.random.fold_in(keys[4], 1), OBS_MAX // 2, OBS_MAX).astype(jnp.int32)
    obs_value = scatter_about(keys[5], (TILES, COLS_TILE, OBS_MAX), 1.0, 6.0, ((0, 16),), jnp.float32)
    obs_rinv = jnp.clip(jnp.exp(math.log(1000.0) - 6.9077553 * jax.random.uniform(keys[6], (TILES, COLS_TILE, OBS_MAX), jnp.float32) ** block_levels(keys[6], (TILES, COLS_TILE, OBS_MAX), ((0, 16),), -0.2, 0.2)), 1.0, 1000.0)
    return {"background": background, "diffusion": diffusion, "advection": advection, "obs_where": obs_where, "obs_count": obs_count, "obs_value": obs_value, "obs_rinv": obs_rinv}


HIGH = lax.Precision.HIGHEST

def analyse(states, where, count, value, rinv):
    members = states.shape[0]
    entries = states.shape[2]
    slots = where.shape[1]
    mean = lax.optimization_barrier(jnp.mean(states, axis=0))
    anomaly = states - mean[None]
    mask = (jnp.arange(slots, dtype=jnp.int32)[None, :] < count[:, None]).astype(jnp.float32)
    onehot = (where[:, :, None] == jnp.arange(entries, dtype=jnp.int32)[None, None, :]).astype(jnp.float32) * mask[:, :, None]
    yb = jnp.einsum('npv,knv->npk', onehot, anomaly, precision=HIGH)
    innov = value - jnp.einsum('npv,nv->np', onehot, mean, precision=HIGH)
    weight_obs = rinv * mask
    eye = jnp.eye(members, dtype=jnp.float32)
    gram = (members - 1.0) * eye[None] + jnp.einsum('npk,npl->nkl', yb * weight_obs[:, :, None], yb, precision=HIGH)
    scale = jnp.sqrt(lax.optimization_barrier(jnp.sum(gram * gram, axis=(1, 2))))
    start_y = gram / scale[:, None, None]
    start_z = jnp.broadcast_to(eye[None], gram.shape)

    def newton(step, carry):
        iter_y, iter_z = carry
        middle = 1.5 * eye[None] - 0.5 * jnp.einsum('nij,njk->nik', iter_z, iter_y, precision=HIGH)
        return (jnp.einsum('nij,njk->nik', iter_y, middle, precision=HIGH), jnp.einsum('nij,njk->nik', middle, iter_z, precision=HIGH))
    final_y, final_z = lax.fori_loop(0, ITERS, newton, (start_y, start_z))
    weights = jnp.sqrt(members - 1.0) * final_z / jnp.sqrt(scale)[:, None, None]
    project = jnp.einsum('npk,np->nk', yb, weight_obs * innov, precision=HIGH)
    inner = jnp.einsum('nkl,nl->nk', final_z, project, precision=HIGH)
    wmean = jnp.einsum('nkl,nl->nk', final_z, inner, precision=HIGH) / scale[:, None]
    trans = weights + wmean[:, :, None]
    return mean[None] + jnp.einsum('nij,inv->jnv', trans, anomaly, precision=HIGH)

def advance(state, diffusion, advection):
    left = jnp.roll(state, 1, axis=1)
    right = jnp.roll(state, -1, axis=1)
    return state + diffusion * (left - 2.0 * state + right) + advection * (0.5 * (left - right))

def reference(background, diffusion, advection, obs_where, obs_count, obs_value, obs_rinv):
    state = background
    for step in range(2):
        state = advance(state, diffusion, advection)
    columns = jnp.transpose(state, (1, 0, 2))
    total = columns.shape[0]
    where = obs_where.reshape(total, -1)
    count = obs_count.reshape(total)
    value = obs_value.reshape(total, -1)
    rinv = obs_rinv.reshape(total, -1)

    def one_column(items):
        column, col_where, col_count, col_value, col_rinv = items
        result = analyse(column[:, None, :], col_where[None], col_count[None], col_value[None], col_rinv[None])
        return result[:, 0, :]
    result = lax.map(one_column, (columns, where, count, value, rinv))
    return jnp.transpose(result, (1, 0, 2))
```

```python
import functools
import math

import jax
import jax.numpy as jnp
from jax import lax
from jax.experimental import pallas as pl
from jax.experimental.pallas import tpu as pltpu
from jax.sharding import PartitionSpec as P

ITERS = 12
F32 = jnp.float32
BF16 = jnp.bfloat16
MESH = pl.DeviceIdType.MESH


def split2(a):
    high = a.astype(BF16)
    return high, (a - high.astype(F32)).astype(BF16)


def split3(a):
    high = a.astype(BF16)
    rest = a - high.astype(F32)
    middle = rest.astype(BF16)
    return high, middle, (rest - middle.astype(F32)).astype(BF16)


def dot(a, b):
    return jnp.dot(a, b, preferred_element_type=F32)


def dot_nt(a, b):
    return lax.dot_general(a, b, (((1,), (1,)), ((), ())), preferred_element_type=F32)


def product(a, b):
    return dot(a[0], b[0]) + (dot(a[0], b[1]) + dot(a[1], b[0]))


def advance(left, middle, right, diffusion, advection):
    return middle + diffusion * (left - 2.0 * middle + right) + advection * (0.5 * (left - right))


def observe(where, count, value, rinv, entries):
    slots = where.shape[1]
    mask = (lax.broadcasted_iota(jnp.int32, (1, slots), 1) < count).astype(F32)
    weight = rinv * mask
    terms = split3(weight) + split3(weight * value)
    row = lax.broadcasted_iota(jnp.int32, (8, slots), 0)
    stacked = jnp.zeros((8, slots), F32)
    for index, term in enumerate(terms):
        stacked = jnp.where(row == index, term.astype(F32), stacked)
    onehot = (lax.broadcasted_iota(jnp.int32, (entries, slots), 0) == where).astype(F32)
    return dot_nt(stacked.astype(BF16), onehot.astype(BF16))


def analyse(states, obs, w_ref, c_ref, members):
    precision = obs[0:1] + (obs[1:2] + obs[2:3])
    target = obs[3:4] + (obs[4:5] + obs[5:6])
    mean = jnp.sum(states, axis=0, keepdims=True) * (1.0 / members)
    anomaly = states - mean
    pull = target - precision * mean
    left = split3(anomaly * precision)
    right = split3(anomaly)
    gram = dot_nt(left[0], right[0]) + (
        (dot_nt(left[0], right[1]) + dot_nt(left[1], right[0]))
        + (dot_nt(left[0], right[2]) + dot_nt(left[2], right[0]) + dot_nt(left[1], right[1]))
    )
    diagonal = lax.broadcasted_iota(jnp.int32, gram.shape, 0) == lax.broadcasted_iota(jnp.int32, gram.shape, 1)
    gram = gram + jnp.where(diagonal, members - 1.0, 0.0)
    square = jnp.sum(jnp.sum(gram * gram, axis=0, keepdims=True), axis=1, keepdims=True)
    scale = jnp.sqrt(square)
    w_ref[...] = gram * (1.0 / scale)
    c_ref[...] = anomaly

    def newton(step, carry):
        iter_w = w_ref[...]
        iter_c = c_ref[...]
        w = split2(iter_w)
        p = 1.5 * iter_w - 0.5 * product(w, w)
        c_ref[...] = 1.5 * iter_c - 0.5 * product(w, split2(iter_c))
        w_ref[...] = 1.5 * p - 0.5 * product(split2(p), w)
        return carry

    lax.fori_loop(0, ITERS - 1, newton, 0)
    iter_c = c_ref[...]
    final = 1.5 * iter_c - 0.5 * product(split2(w_ref[...]), split2(iter_c))
    inner = jnp.sum(final * pull, axis=1, keepdims=True)
    shift = jnp.sum(final * inner, axis=0, keepdims=True) * (1.0 / scale)
    coefficient = math.sqrt(members - 1.0) / jnp.sqrt(scale)
    return (mean + shift) + coefficient * final


def kernel(
    groups, tiles, bg_ref, diff_ref, adv_ref, where_ref, count_ref, value_ref, rinv_ref, out_ref,
    ext, sent, owned, result, obs, w_ref, c_ref,
    load_sem, halo_send, halo_recv, gather_send, gather_recv, back_send, back_recv,
):
    me = lax.axis_index("mem")
    tile = lax.axis_index("tile")
    cols, local, entries = sent.shape
    chunks = cols // groups
    members = groups * local
    right, left = lax.rem(tile + 1, tiles), lax.rem(tile + tiles - 1, tiles)

    load = pltpu.make_async_copy(bg_ref, ext.at[pl.ds(2, cols)], load_sem)
    load.start()
    barrier = pltpu.get_barrier_semaphore()

    def greet(step, carry):
        peer = lax.rem(me + step, groups)
        pl.semaphore_signal(barrier, inc=1, device_id={"mem": peer}, device_id_type=MESH)
        return carry

    lax.fori_loop(1, groups, greet, 0)
    for neighbour in (left, right):
        pl.semaphore_signal(barrier, inc=1, device_id={"tile": neighbour}, device_id_type=MESH)
    diffusion = diff_ref[...]
    advection = adv_ref[...]
    load.wait()
    pl.semaphore_wait(barrier, groups + 1)

    tail = pltpu.make_async_remote_copy(
        src_ref=ext.at[pl.ds(cols, 2)], dst_ref=ext.at[pl.ds(0, 2)], send_sem=halo_send.at[0], recv_sem=halo_recv.at[0],
        device_id={"tile": right}, device_id_type=MESH)
    head = pltpu.make_async_remote_copy(
        src_ref=ext.at[pl.ds(2, 2)], dst_ref=ext.at[pl.ds(cols + 2, 2)], send_sem=halo_send.at[1], recv_sem=halo_recv.at[1],
        device_id={"tile": left}, device_id_type=MESH)
    tail.start()
    head.start()

    def forecast(chunk):
        base = chunk * groups
        width = min(8, groups)
        for start in range(base, base + groups, width):
            cells = ext[start:start + width + 4]
            half = advance(cells[:-2], cells[1:-1], cells[2:], diffusion, advection)
            sent[start:start + width] = advance(half[:-2], half[1:-1], half[2:], diffusion, advection)

    mine = pl.ds(pl.multiple_of(me * local, local), local)

    def scatter(chunk):
        owned[chunk, mine, :] = sent[chunk * groups + me]

        def send(step, carry):
            peer = lax.rem(me + step, groups)
            pltpu.make_async_remote_copy(
                src_ref=sent.at[chunk * groups + peer], dst_ref=owned.at[chunk, mine],
                send_sem=gather_send.at[chunk], recv_sem=gather_recv.at[chunk],
                device_id={"mem": peer}, device_id_type=MESH).start()
            return carry

        lax.fori_loop(1, groups, send, 0)

    for chunk in range(1, chunks - 1):
        forecast(chunk)
        scatter(chunk)
    tail.wait()
    head.wait()
    for chunk in (chunks - 1, 0):
        forecast(chunk)
        scatter(chunk)

    for chunk in range(chunks):
        row = pl.ds(chunk * groups + me, 1)
        lanes = lax.broadcasted_iota(jnp.int32, count_ref.shape, 1)
        count = jnp.sum(jnp.where(lanes == chunk * groups + me, count_ref[...], 0), axis=1, keepdims=True)
        obs[chunk] = observe(where_ref[row, :], count, value_ref[row, :], rinv_ref[row, :], entries)

    bulk = (groups - 1) * local

    def column(step, carry):
        chunk = lax.rem(step + 1, chunks)
        pltpu.make_async_remote_copy(
            src_ref=owned.at[chunk, pl.ds(0, bulk)], dst_ref=owned.at[chunk, pl.ds(0, bulk)],
            send_sem=gather_send.at[chunk], recv_sem=gather_recv.at[chunk],
            device_id={"mem": me}, device_id_type=MESH).wait_recv()
        result[chunk] = analyse(owned[chunk], obs[chunk], w_ref, c_ref, members)
        at = chunk * groups + me

        def send(hop, inner):
            peer = lax.rem(me + hop, groups)
            pltpu.make_async_remote_copy(
                src_ref=result.at[chunk, pl.ds(pl.multiple_of(peer * local, local), local)], dst_ref=out_ref.at[at],
                send_sem=back_send.at[chunk], recv_sem=back_recv.at[chunk],
                device_id={"mem": peer}, device_id_type=MESH).start()
            return inner

        lax.fori_loop(1, groups, send, 0)
        out_ref[at] = result[chunk, mine, :]
        return carry

    lax.fori_loop(0, chunks, column, 0)
    for chunk in range(chunks):
        pltpu.make_async_remote_copy(
            src_ref=owned.at[chunk, pl.ds(0, bulk)], dst_ref=owned.at[chunk, pl.ds(0, bulk)],
            send_sem=gather_send.at[chunk], recv_sem=gather_recv.at[chunk],
            device_id={"mem": me}, device_id_type=MESH).wait_send()
        pltpu.make_async_remote_copy(
            src_ref=out_ref.at[pl.ds(0, groups - 1)], dst_ref=out_ref.at[pl.ds(0, groups - 1)],
            send_sem=back_send.at[chunk], recv_sem=back_recv.at[chunk],
            device_id={"mem": me}, device_id_type=MESH).wait()


def body(groups, tiles, background, diffusion, advection, obs_where, obs_count, obs_value, obs_rinv):
    local, cols, entries = background.shape
    chunks = cols // groups
    members = local * groups
    vmem = pl.BlockSpec(memory_space=pltpu.VMEM)
    result = pl.pallas_call(
        functools.partial(kernel, groups, tiles),
        out_shape=jax.ShapeDtypeStruct((cols, local, entries), F32),
        in_specs=[pl.BlockSpec(memory_space=pl.ANY)] + [vmem] * 6,
        out_specs=vmem,
        scratch_shapes=[
            pltpu.VMEM((cols + 4, local, entries), F32),
            pltpu.VMEM((cols, local, entries), F32),
            pltpu.VMEM((chunks, members, entries), F32),
            pltpu.VMEM((chunks, members, entries), F32),
            pltpu.VMEM((chunks, 8, entries), F32),
            pltpu.VMEM((members, members), F32),
            pltpu.VMEM((members, entries), F32),
            pltpu.SemaphoreType.DMA,
            pltpu.SemaphoreType.DMA((2,)),
            pltpu.SemaphoreType.DMA((2,)),
            pltpu.SemaphoreType.DMA((chunks,)),
            pltpu.SemaphoreType.DMA((chunks,)),
            pltpu.SemaphoreType.DMA((chunks,)),
            pltpu.SemaphoreType.DMA((chunks,)),
        ],
        compiler_params=pltpu.CompilerParams(collective_id=0, has_side_effects=True, vmem_limit_bytes=48 << 20),
    )(
        jnp.transpose(background, (1, 0, 2)), diffusion[None, :], advection[None, :],
        obs_where[0], obs_count, obs_value[0], obs_rinv[0],
    )
    return jnp.transpose(result, (1, 0, 2))


def solution(mesh):
    return jax.shard_map(
        functools.partial(body, mesh.shape["mem"], mesh.shape["tile"]),
        mesh=mesh,
        in_specs=(
            P("mem", "tile", None),
            P(),
            P(),
            P("tile", None, None),
            P("tile", None),
            P("tile", None, None),
            P("tile", None, None),
        ),
        out_specs=P("mem", "tile", None),
        check_vma=False,
    )
```

```python
import functools
import math

import jax
import jax.numpy as jnp
from jax import lax
from jax.experimental import pallas as pl
from jax.experimental.pallas import tpu as pltpu
from jax.sharding import PartitionSpec as P

ITERS = 12
F32 = jnp.float32
BF16 = jnp.bfloat16
MESH = pl.DeviceIdType.MESH


def split2(a):
    high = a.astype(BF16)
    return high, (a - high.astype(F32)).astype(BF16)


def split3(a):
    high = a.astype(BF16)
    rest = a - high.astype(F32)
    middle = rest.astype(BF16)
    return high, middle, (rest - middle.astype(F32)).astype(BF16)


def dot(a, b):
    return jnp.dot(a, b, preferred_element_type=F32)


def dot_nt(a, b):
    return lax.dot_general(a, b, (((1,), (1,)), ((), ())), preferred_element_type=F32)


def product(a, b):
    return dot(a[0], b[0]) + (dot(a[0], b[1]) + dot(a[1], b[0]))


def advance(left, middle, right, diffusion, advection):
    return middle + diffusion * (left - 2.0 * middle + right) + advection * (0.5 * (left - right))


def observe(where, count, value, rinv, entries):
    slots = where.shape[1]
    mask = (lax.broadcasted_iota(jnp.int32, (1, slots), 1) < count).astype(F32)
    weight = rinv * mask
    terms = split3(weight) + split3(weight * value)
    row = lax.broadcasted_iota(jnp.int32, (8, slots), 0)
    stacked = jnp.zeros((8, slots), F32)
    for index, term in enumerate(terms):
        stacked = jnp.where(row == index, term.astype(F32), stacked)
    onehot = (lax.broadcasted_iota(jnp.int32, (entries, slots), 0) == where).astype(F32)
    return dot_nt(stacked.astype(BF16), onehot.astype(BF16))


def analyse(states, obs, w_ref, c_ref, members):
    precision = obs[0:1] + (obs[1:2] + obs[2:3])
    target = obs[3:4] + (obs[4:5] + obs[5:6])
    mean = jnp.sum(states, axis=0, keepdims=True) * (1.0 / members)
    anomaly = states - mean
    pull = target - precision * mean
    left = split3(anomaly * precision)
    right = split3(anomaly)
    gram = dot_nt(left[0], right[0]) + (
        (dot_nt(left[0], right[1]) + dot_nt(left[1], right[0]))
        + (dot_nt(left[0], right[2]) + dot_nt(left[2], right[0]) + dot_nt(left[1], right[1]))
    )
    diagonal = lax.broadcasted_iota(jnp.int32, gram.shape, 0) == lax.broadcasted_iota(jnp.int32, gram.shape, 1)
    gram = gram + jnp.where(diagonal, members - 1.0, 0.0)
    square = jnp.sum(jnp.sum(gram * gram, axis=0, keepdims=True), axis=1, keepdims=True)
    scale = jnp.sqrt(square)
    w_ref[...] = gram * (1.0 / scale)
    c_ref[...] = anomaly

    def newton(step, carry):
        iter_w = w_ref[...]
        iter_c = c_ref[...]
        w = split2(iter_w)
        p = 1.5 * iter_w - 0.5 * product(w, w)
        c_ref[...] = 1.5 * iter_c - 0.5 * product(w, split2(iter_c))
        w_ref[...] = 1.5 * p - 0.5 * product(split2(p), w)
        return carry

    lax.fori_loop(0, ITERS - 1, newton, 0)
    iter_c = c_ref[...]
    final = 1.5 * iter_c - 0.5 * product(split2(w_ref[...]), split2(iter_c))
    inner = jnp.sum(final * pull, axis=1, keepdims=True)
    shift = jnp.sum(final * inner, axis=0, keepdims=True) * (1.0 / scale)
    coefficient = math.sqrt(members - 1.0) / jnp.sqrt(scale)
    return (mean + shift) + coefficient * final


ZERO, HEAD, TILE, LATE = 0, 1, 2, 3


def kernel(
    groups, tiles, bg_ref, diff_ref, adv_ref, where_ref, count_ref, value_ref, rinv_ref, out_ref,
    ext, sent, owned, result, obs, where, value, rinv, diff, adv, counts, w_ref, c_ref,
    load_sem, halo_send, halo_recv, gather_send, gather_recv, back_send, back_recv, go_sem, first_sem, tile_sem,
):
    me = lax.axis_index("mem")
    tile = lax.axis_index("tile")
    cols, local, entries = sent.shape
    chunks = cols // groups
    members = groups * local
    right, left = lax.rem(tile + 1, tiles), lax.rem(tile + tiles - 1, tiles)

    loads = [
        pltpu.make_async_copy(bg_ref.at[index], ext.at[pl.ds(2, cols), index], load_sem.at[index])
        for index in range(local)
    ]
    small = ((diff_ref, diff), (adv_ref, adv), (count_ref, counts), (where_ref, where), (value_ref, value), (rinv_ref, rinv))
    loads += [
        pltpu.make_async_copy(source, target, load_sem.at[local + index]) for index, (source, target) in enumerate(small)
    ]
    for load in loads:
        load.start()
    barrier = pltpu.get_barrier_semaphore()

    def peers(action):
        def visit(step, carry):
            action(lax.rem(me + step, groups))
            return carry

        lax.fori_loop(1, groups, visit, 0)

    def tell(semaphore, peer, **where_to):
        pl.semaphore_signal(semaphore, inc=1, device_id={"mem": peer, **where_to}, device_id_type=MESH)

    @pl.when(me == ZERO)
    def _():
        tell(barrier, LATE)

    @pl.when(me != ZERO)
    def _():
        peers(lambda peer: pl.when((peer == HEAD) | (peer > LATE))(lambda: tell(barrier, peer)))

    @pl.when((me == HEAD) | (me > LATE))
    def _():
        pl.semaphore_wait(barrier, groups - 2)

    @pl.when(me == HEAD)
    def _():
        tell(go_sem, TILE)
        tell(go_sem, LATE)

    @pl.when((me == TILE) | (me == LATE))
    def _():
        pl.semaphore_wait(go_sem, 1)

    @pl.when(me == ZERO)
    def _():
        pl.semaphore_wait(first_sem, 1)

    for load in loads[:local + 2]:
        load.wait()
    diffusion = diff[...]
    advection = adv[...]

    def forecast(begin, end):
        width = min(8, groups)
        for start in range(begin, end, width):
            stop = min(start + width, end)
            cells = ext[start:stop + 4]
            half = advance(cells[:-2], cells[1:-1], cells[2:], diffusion, advection)
            sent[start:stop] = advance(half[:-2], half[1:-1], half[2:], diffusion, advection)

    mine = pl.ds(pl.multiple_of(me * local, local), local)

    def hand_over(chunk, peer):
        pltpu.make_async_remote_copy(
            src_ref=sent.at[chunk * groups + peer], dst_ref=owned.at[chunk, mine],
            send_sem=gather_send.at[chunk], recv_sem=gather_recv.at[chunk],
            device_id={"mem": peer}, device_id_type=MESH).start()

    def keep(chunk):
        owned[chunk, mine, :] = sent[chunk * groups + me]

    last = chunks - 1
    forecast(groups, 2 * groups)
    keep(1)
    peers(lambda peer: pl.when(peer != ZERO)(lambda: hand_over(1, peer)))

    @pl.when(me == LATE)
    def _():
        pl.semaphore_wait(barrier, 1)
        peers(lambda peer: tell(first_sem, peer))
        tell(barrier, TILE, tile=left)
        tell(barrier, TILE, tile=right)

    @pl.when((me != LATE) & (me != ZERO))
    def _():
        pl.semaphore_wait(first_sem, 1)

    @pl.when(me != ZERO)
    def _():
        hand_over(1, ZERO)

    for chunk in range(2, last):
        forecast(chunk * groups, (chunk + 1) * groups)
        keep(chunk)
        peers(lambda peer: hand_over(chunk, peer))
    forecast(last * groups, cols - 2)
    peers(lambda peer: pl.when(peer < groups - 2)(lambda: hand_over(last, peer)))
    forecast(2, groups)
    peers(lambda peer: pl.when(peer > 1)(lambda: hand_over(0, peer)))

    for load in loads[local + 2:]:
        load.wait()
    for chunk in range(chunks):
        row = pl.ds(chunk * groups + me, 1)
        lanes = lax.broadcasted_iota(jnp.int32, counts.shape, 1)
        count = jnp.sum(jnp.where(lanes == chunk * groups + me, counts[...], 0), axis=1, keepdims=True)
        obs[chunk] = observe(where[row, :], count, value[row, :], rinv[row, :], entries)

    tail = pltpu.make_async_remote_copy(
        src_ref=ext.at[pl.ds(cols, 2)], dst_ref=ext.at[pl.ds(0, 2)], send_sem=halo_send.at[0], recv_sem=halo_recv.at[0],
        device_id={"tile": right}, device_id_type=MESH)
    head = pltpu.make_async_remote_copy(
        src_ref=ext.at[pl.ds(2, 2)], dst_ref=ext.at[pl.ds(cols + 2, 2)], send_sem=halo_send.at[1], recv_sem=halo_recv.at[1],
        device_id={"tile": left}, device_id_type=MESH)

    def exchange_edges():
        @pl.when(me == TILE)
        def _():
            pl.semaphore_wait(barrier, 2)
            peers(lambda peer: tell(tile_sem, peer))

        @pl.when(me != TILE)
        def _():
            pl.semaphore_wait(tile_sem, 1)

        tail.start()
        head.start()

    def send_edges():
        tail.wait()
        head.wait()
        forecast(0, 2)
        forecast(cols - 2, cols)
        keep(0)
        keep(last)
        for chunk, owner in ((last, groups - 2), (last, groups - 1), (0, 0), (0, 1)):
            pl.when(me != owner)(functools.partial(hand_over, chunk, owner))

    bulk = (groups - 1) * local

    def column(step, carry):
        chunk = lax.rem(step + 1, chunks)
        pl.when(step == 2)(send_edges)
        pltpu.make_async_remote_copy(
            src_ref=owned.at[chunk, pl.ds(0, bulk)], dst_ref=owned.at[chunk, pl.ds(0, bulk)],
            send_sem=gather_send.at[chunk], recv_sem=gather_recv.at[chunk],
            device_id={"mem": me}, device_id_type=MESH).wait_recv()
        result[chunk] = analyse(owned[chunk], obs[chunk], w_ref, c_ref, members)
        at = chunk * groups + me
        peers(lambda peer: pltpu.make_async_remote_copy(
            src_ref=result.at[chunk, pl.ds(pl.multiple_of(peer * local, local), local)], dst_ref=out_ref.at[at],
            send_sem=back_send.at[chunk], recv_sem=back_recv.at[chunk],
            device_id={"mem": peer}, device_id_type=MESH).start())
        out_ref[at] = result[chunk, mine, :]
        pl.when(step == 0)(exchange_edges)
        return carry

    lax.fori_loop(0, chunks, column, 0)
    for chunk in range(chunks):
        pltpu.make_async_remote_copy(
            src_ref=owned.at[chunk, pl.ds(0, bulk)], dst_ref=owned.at[chunk, pl.ds(0, bulk)],
            send_sem=gather_send.at[chunk], recv_sem=gather_recv.at[chunk],
            device_id={"mem": me}, device_id_type=MESH).wait_send()
        pltpu.make_async_remote_copy(
            src_ref=out_ref.at[pl.ds(0, groups - 1)], dst_ref=out_ref.at[pl.ds(0, groups - 1)],
            send_sem=back_send.at[chunk], recv_sem=back_recv.at[chunk],
            device_id={"mem": me}, device_id_type=MESH).wait()


def body(groups, tiles, background, diffusion, advection, obs_where, obs_count, obs_value, obs_rinv):
    local, cols, entries = background.shape
    chunks = cols // groups
    members = local * groups
    vmem = pl.BlockSpec(memory_space=pltpu.VMEM)
    hbm = pl.BlockSpec(memory_space=pltpu.HBM)
    slots = obs_where.shape[2]
    result = pl.pallas_call(
        functools.partial(kernel, groups, tiles),
        out_shape=pltpu.VMEM((cols, local, entries), F32),
        in_specs=[hbm] * 7,
        out_specs=vmem,
        scratch_shapes=[
            pltpu.VMEM((cols + 4, local, entries), F32),
            pltpu.VMEM((cols, local, entries), F32),
            pltpu.VMEM((chunks, members, entries), F32),
            pltpu.VMEM((chunks, members, entries), F32),
            pltpu.VMEM((chunks, 8, entries), F32),
            pltpu.VMEM((cols, slots), jnp.int32),
            pltpu.VMEM((cols, slots), F32),
            pltpu.VMEM((cols, slots), F32),
            pltpu.VMEM((1, entries), F32),
            pltpu.VMEM((1, entries), F32),
            pltpu.VMEM((1, cols), jnp.int32),
            pltpu.VMEM((members, members), F32),
            pltpu.VMEM((members, entries), F32),
            pltpu.SemaphoreType.DMA((local + 6,)),
            pltpu.SemaphoreType.DMA((2,)),
            pltpu.SemaphoreType.DMA((2,)),
            pltpu.SemaphoreType.DMA((chunks,)),
            pltpu.SemaphoreType.DMA((chunks,)),
            pltpu.SemaphoreType.DMA((chunks,)),
            pltpu.SemaphoreType.DMA((chunks,)),
            pltpu.SemaphoreType.REGULAR,
            pltpu.SemaphoreType.REGULAR,
            pltpu.SemaphoreType.REGULAR,
        ],
        compiler_params=pltpu.CompilerParams(collective_id=0, has_side_effects=True, vmem_limit_bytes=48 << 20),
    )(*(
        pltpu.with_memory_space_constraint(operand, pltpu.HBM)
        for operand in (
            background, diffusion[None, :], advection[None, :], obs_where[0], obs_count, obs_value[0], obs_rinv[0],
        )
    ))
    return jnp.transpose(result, (1, 0, 2))


def solution(mesh):
    return jax.shard_map(
        functools.partial(body, mesh.shape["mem"], mesh.shape["tile"]),
        mesh=mesh,
        in_specs=(
            P("mem", "tile", None),
            P(),
            P(),
            P("tile", None, None),
            P("tile", None),
            P("tile", None, None),
            P("tile", None, None),
        ),
        out_specs=P("mem", "tile", None),
        check_vma=False,
    )
```

```python
import functools
import math

import jax
import jax.numpy as jnp
from jax import lax
from jax.experimental import pallas as pl
from jax.experimental.pallas import tpu as pltpu
from jax.sharding import PartitionSpec as P

ITERS = 12
F32 = jnp.float32
BF16 = jnp.bfloat16
MESH = pl.DeviceIdType.MESH


def split2(a):
    high = a.astype(BF16)
    return high, (a - high.astype(F32)).astype(BF16)


def split3(a):
    high = a.astype(BF16)
    rest = a - high.astype(F32)
    middle = rest.astype(BF16)
    return high, middle, (rest - middle.astype(F32)).astype(BF16)


def dot(a, b):
    return jnp.dot(a, b, preferred_element_type=F32)


def dot_nt(a, b):
    return lax.dot_general(a, b, (((1,), (1,)), ((), ())), preferred_element_type=F32)


def product(a, b):
    return dot(a[0], b[0]) + (dot(a[0], b[1]) + dot(a[1], b[0]))


def advance(left, middle, right, diffusion, advection):
    return middle + diffusion * (left - 2.0 * middle + right) + advection * (0.5 * (left - right))


def observe(where, count, value, rinv, entries):
    slots = where.shape[1]
    mask = (lax.broadcasted_iota(jnp.int32, (1, slots), 1) < count).astype(F32)
    weight = rinv * mask
    terms = split3(weight) + split3(weight * value)
    row = lax.broadcasted_iota(jnp.int32, (8, slots), 0)
    stacked = jnp.zeros((8, slots), F32)
    for index, term in enumerate(terms):
        stacked = jnp.where(row == index, term.astype(F32), stacked)
    onehot = (lax.broadcasted_iota(jnp.int32, (entries, slots), 0) == where).astype(F32)
    return dot_nt(stacked.astype(BF16), onehot.astype(BF16))


def analyse(states, obs, w_ref, c_ref, members):
    precision = obs[0:1] + (obs[1:2] + obs[2:3])
    target = obs[3:4] + (obs[4:5] + obs[5:6])
    mean = jnp.sum(states, axis=0, keepdims=True) * (1.0 / members)
    anomaly = states - mean
    pull = target - precision * mean
    left = split3(anomaly * precision)
    right = split3(anomaly)
    gram = dot_nt(left[0], right[0]) + (
        (dot_nt(left[0], right[1]) + dot_nt(left[1], right[0]))
        + (dot_nt(left[0], right[2]) + dot_nt(left[2], right[0]) + dot_nt(left[1], right[1]))
    )
    diagonal = lax.broadcasted_iota(jnp.int32, gram.shape, 0) == lax.broadcasted_iota(jnp.int32, gram.shape, 1)
    gram = gram + jnp.where(diagonal, members - 1.0, 0.0)
    square = jnp.sum(jnp.sum(gram * gram, axis=0, keepdims=True), axis=1, keepdims=True)
    scale = jnp.sqrt(square)
    w_ref[...] = gram * (1.0 / scale)
    c_ref[...] = anomaly

    def newton(step, carry):
        iter_w = w_ref[...]
        iter_c = c_ref[...]
        w = split2(iter_w)
        p = 1.5 * iter_w - 0.5 * product(w, w)
        c_ref[...] = 1.5 * iter_c - 0.5 * product(w, split2(iter_c))
        w_ref[...] = 1.5 * p - 0.5 * product(split2(p), w)
        return carry

    lax.fori_loop(0, ITERS - 1, newton, 0)
    iter_c = c_ref[...]
    final = 1.5 * iter_c - 0.5 * product(split2(w_ref[...]), split2(iter_c))
    inner = jnp.sum(final * pull, axis=1, keepdims=True)
    shift = jnp.sum(final * inner, axis=0, keepdims=True) * (1.0 / scale)
    coefficient = math.sqrt(members - 1.0) / jnp.sqrt(scale)
    return (mean + shift) + coefficient * final


ZERO, HEAD, TILE, LATE = 0, 1, 2, 3


def kernel(
    groups, tiles, bg_ref, diff_ref, adv_ref, where_ref, count_ref, value_ref, rinv_ref, out_ref,
    ext, sent, owned, result, obs, where, value, rinv, diff, adv, counts, w_ref, c_ref,
    load_sem, halo_send, halo_recv, gather_send, gather_recv, back_send, back_recv, go_sem, first_sem, tile_sem,
):
    me = lax.axis_index("mem")
    tile = lax.axis_index("tile")
    cols, local, entries = sent.shape
    chunks = cols // groups
    members = groups * local
    right, left = lax.rem(tile + 1, tiles), lax.rem(tile + tiles - 1, tiles)

    loads = [
        pltpu.make_async_copy(bg_ref.at[index], ext.at[pl.ds(2, cols), index], load_sem.at[index])
        for index in range(local)
    ]
    small = ((diff_ref, diff), (adv_ref, adv), (count_ref, counts), (where_ref, where), (value_ref, value), (rinv_ref, rinv))
    loads += [
        pltpu.make_async_copy(source, target, load_sem.at[local + index]) for index, (source, target) in enumerate(small)
    ]
    for load in loads:
        load.start()
    barrier = pltpu.get_barrier_semaphore()

    def peers(action):
        def visit(step, carry):
            action(lax.rem(me + step, groups))
            return carry

        lax.fori_loop(1, groups, visit, 0)

    def tell(semaphore, peer, **where_to):
        pl.semaphore_signal(semaphore, inc=1, device_id={"mem": peer, **where_to}, device_id_type=MESH)

    @pl.when(me == ZERO)
    def _():
        tell(barrier, LATE)

    @pl.when(me != ZERO)
    def _():
        peers(lambda peer: pl.when((peer == HEAD) | (peer > LATE))(lambda: tell(barrier, peer)))

    @pl.when((me == HEAD) | (me > LATE))
    def _():
        pl.semaphore_wait(barrier, groups - 2)

    @pl.when(me == HEAD)
    def _():
        tell(go_sem, TILE)
        tell(go_sem, LATE)

    @pl.when((me == TILE) | (me == LATE))
    def _():
        pl.semaphore_wait(go_sem, 1)

    @pl.when(me == ZERO)
    def _():
        pl.semaphore_wait(first_sem, 1)

    for load in loads[:local + 2]:
        load.wait()
    diffusion = diff[...]
    advection = adv[...]

    def forecast(begin, end):
        width = min(8, groups)
        for start in range(begin, end, width):
            stop = min(start + width, end)
            cells = ext[start:stop + 4]
            half = advance(cells[:-2], cells[1:-1], cells[2:], diffusion, advection)
            sent[start:stop] = advance(half[:-2], half[1:-1], half[2:], diffusion, advection)

    mine = pl.ds(pl.multiple_of(me * local, local), local)

    def hand_over(chunk, peer):
        pltpu.make_async_remote_copy(
            src_ref=sent.at[chunk * groups + peer], dst_ref=owned.at[chunk, mine],
            send_sem=gather_send.at[chunk], recv_sem=gather_recv.at[chunk],
            device_id={"mem": peer}, device_id_type=MESH).start()

    def keep(chunk):
        owned[chunk, mine, :] = sent[chunk * groups + me]

    last = chunks - 1
    forecast(groups, 2 * groups)
    keep(1)
    peers(lambda peer: pl.when(peer != ZERO)(lambda: hand_over(1, peer)))

    @pl.when(me == LATE)
    def _():
        pl.semaphore_wait(barrier, 1)
        peers(lambda peer: tell(first_sem, peer))
        tell(barrier, TILE, tile=left)
        tell(barrier, TILE, tile=right)

    @pl.when((me != LATE) & (me != ZERO))
    def _():
        pl.semaphore_wait(first_sem, 1)

    @pl.when(me != ZERO)
    def _():
        hand_over(1, ZERO)

    for chunk in range(2, last):
        forecast(chunk * groups, (chunk + 1) * groups)
        keep(chunk)
        peers(lambda peer: hand_over(chunk, peer))
    forecast(last * groups, cols - 2)
    peers(lambda peer: pl.when(peer < groups - 2)(lambda: hand_over(last, peer)))
    forecast(2, groups)
    peers(lambda peer: pl.when(peer > 1)(lambda: hand_over(0, peer)))

    for load in loads[local + 2:]:
        load.wait()
    for chunk in range(chunks):
        row = pl.ds(chunk * groups + me, 1)
        lanes = lax.broadcasted_iota(jnp.int32, counts.shape, 1)
        count = jnp.sum(jnp.where(lanes == chunk * groups + me, counts[...], 0), axis=1, keepdims=True)
        obs[chunk] = observe(where[row, :], count, value[row, :], rinv[row, :], entries)

    tail = pltpu.make_async_remote_copy(
        src_ref=ext.at[pl.ds(cols, 2)], dst_ref=ext.at[pl.ds(0, 2)], send_sem=halo_send.at[0], recv_sem=halo_recv.at[0],
        device_id={"tile": right}, device_id_type=MESH)
    head = pltpu.make_async_remote_copy(
        src_ref=ext.at[pl.ds(2, 2)], dst_ref=ext.at[pl.ds(cols + 2, 2)], send_sem=halo_send.at[1], recv_sem=halo_recv.at[1],
        device_id={"tile": left}, device_id_type=MESH)

    def exchange_edges():
        @pl.when(me == TILE)
        def _():
            pl.semaphore_wait(barrier, 2)
            peers(lambda peer: tell(tile_sem, peer))

        @pl.when(me != TILE)
        def _():
            pl.semaphore_wait(tile_sem, 1)

        tail.start()
        head.start()

    def send_edges():
        tail.wait()
        head.wait()
        forecast(0, 2)
        forecast(cols - 2, cols)
        keep(0)
        keep(last)
        for chunk, owner in ((last, groups - 2), (last, groups - 1), (0, 0), (0, 1)):
            pl.when(me != owner)(functools.partial(hand_over, chunk, owner))

    bulk = (groups - 1) * local

    def column(step, carry):
        chunk = lax.rem(step + 1, chunks)
        chunk = jnp.where((me >= groups // 2) & (step >= last - 1), (step - (last - 1)) * last, chunk)
        pl.when(step == last - 1)(send_edges)
        pltpu.make_async_remote_copy(
            src_ref=owned.at[chunk, pl.ds(0, bulk)], dst_ref=owned.at[chunk, pl.ds(0, bulk)],
            send_sem=gather_send.at[chunk], recv_sem=gather_recv.at[chunk],
            device_id={"mem": me}, device_id_type=MESH).wait_recv()
        result[chunk] = analyse(owned[chunk], obs[chunk], w_ref, c_ref, members)
        at = chunk * groups + me
        peers(lambda peer: pltpu.make_async_remote_copy(
            src_ref=result.at[chunk, pl.ds(pl.multiple_of(peer * local, local), local)], dst_ref=out_ref.at[at],
            send_sem=back_send.at[chunk], recv_sem=back_recv.at[chunk],
            device_id={"mem": peer}, device_id_type=MESH).start())
        out_ref[at] = result[chunk, mine, :]
        pl.when((step == 0) & (tile == 0))(exchange_edges)
        return carry

    pl.when(tile != 0)(exchange_edges)
    lax.fori_loop(0, chunks, column, 0)
    for chunk in range(chunks):
        pltpu.make_async_remote_copy(
            src_ref=owned.at[chunk, pl.ds(0, bulk)], dst_ref=owned.at[chunk, pl.ds(0, bulk)],
            send_sem=gather_send.at[chunk], recv_sem=gather_recv.at[chunk],
            device_id={"mem": me}, device_id_type=MESH).wait_send()
        pltpu.make_async_remote_copy(
            src_ref=out_ref.at[pl.ds(0, groups - 1)], dst_ref=out_ref.at[pl.ds(0, groups - 1)],
            send_sem=back_send.at[chunk], recv_sem=back_recv.at[chunk],
            device_id={"mem": me}, device_id_type=MESH).wait()


def body(groups, tiles, background, diffusion, advection, obs_where, obs_count, obs_value, obs_rinv):
    local, cols, entries = background.shape
    chunks = cols // groups
    members = local * groups
    vmem = pl.BlockSpec(memory_space=pltpu.VMEM)
    hbm = pl.BlockSpec(memory_space=pltpu.HBM)
    slots = obs_where.shape[2]
    result = pl.pallas_call(
        functools.partial(kernel, groups, tiles),
        out_shape=pltpu.VMEM((cols, local, entries), F32),
        in_specs=[hbm] * 7,
        out_specs=vmem,
        scratch_shapes=[
            pltpu.VMEM((cols + 4, local, entries), F32),
            pltpu.VMEM((cols, local, entries), F32),
            pltpu.VMEM((chunks, members, entries), F32),
            pltpu.VMEM((chunks, members, entries), F32),
            pltpu.VMEM((chunks, 8, entries), F32),
            pltpu.VMEM((cols, slots), jnp.int32),
            pltpu.VMEM((cols, slots), F32),
            pltpu.VMEM((cols, slots), F32),
            pltpu.VMEM((1, entries), F32),
            pltpu.VMEM((1, entries), F32),
            pltpu.VMEM((1, cols), jnp.int32),
            pltpu.VMEM((members, members), F32),
            pltpu.VMEM((members, entries), F32),
            pltpu.SemaphoreType.DMA((local + 6,)),
            pltpu.SemaphoreType.DMA((2,)),
            pltpu.SemaphoreType.DMA((2,)),
            pltpu.SemaphoreType.DMA((chunks,)),
            pltpu.SemaphoreType.DMA((chunks,)),
            pltpu.SemaphoreType.DMA((chunks,)),
            pltpu.SemaphoreType.DMA((chunks,)),
            pltpu.SemaphoreType.REGULAR,
            pltpu.SemaphoreType.REGULAR,
            pltpu.SemaphoreType.REGULAR,
        ],
        compiler_params=pltpu.CompilerParams(collective_id=0, has_side_effects=True, vmem_limit_bytes=48 << 20),
    )(*(
        pltpu.with_memory_space_constraint(operand, pltpu.HBM)
        for operand in (
            background, diffusion[None, :], advection[None, :], obs_where[0], obs_count, obs_value[0], obs_rinv[0],
        )
    ))
    return jnp.transpose(result, (1, 0, 2))


def solution(mesh):
    return jax.shard_map(
        functools.partial(body, mesh.shape["mem"], mesh.shape["tile"]),
        mesh=mesh,
        in_specs=(
            P("mem", "tile", None),
            P(),
            P(),
            P("tile", None, None),
            P("tile", None),
            P("tile", None, None),
            P("tile", None, None),
        ),
        out_specs=P("mem", "tile", None),
        check_vma=False,
    )
```

```python
import functools
import math

import jax
import jax.numpy as jnp
from jax import lax
from jax.experimental import pallas as pl
from jax.experimental.pallas import tpu as pltpu
from jax.sharding import PartitionSpec as P

ITERS = 12
F32 = jnp.float32
BF16 = jnp.bfloat16
MESH = pl.DeviceIdType.MESH


def split2(a):
    high = a.astype(BF16)
    return high, (a - high.astype(F32)).astype(BF16)


def split3(a):
    high = a.astype(BF16)
    rest = a - high.astype(F32)
    middle = rest.astype(BF16)
    return high, middle, (rest - middle.astype(F32)).astype(BF16)


def dot(a, b):
    return jnp.dot(a, b, preferred_element_type=F32)


def dot_nt(a, b):
    return lax.dot_general(a, b, (((1,), (1,)), ((), ())), preferred_element_type=F32)


def product(a, b):
    return dot(a[0], b[0]) + (dot(a[0], b[1]) + dot(a[1], b[0]))


def advance(left, middle, right, diffusion, advection):
    return middle + diffusion * (left - 2.0 * middle + right) + advection * (0.5 * (left - right))


def observe(where, count, value, rinv, entries):
    slots = where.shape[1]
    mask = (lax.broadcasted_iota(jnp.int32, (1, slots), 1) < count).astype(F32)
    weight = rinv * mask
    terms = split3(weight) + split3(weight * value)
    row = lax.broadcasted_iota(jnp.int32, (8, slots), 0)
    stacked = jnp.zeros((8, slots), F32)
    for index, term in enumerate(terms):
        stacked = jnp.where(row == index, term.astype(F32), stacked)
    onehot = (lax.broadcasted_iota(jnp.int32, (entries, slots), 0) == where).astype(F32)
    return dot_nt(stacked.astype(BF16), onehot.astype(BF16))


def analyse(states, obs, w_ref, c_ref, s_ref, members, halfway):
    precision = obs[0:1] + (obs[1:2] + obs[2:3])
    target = obs[3:4] + (obs[4:5] + obs[5:6])
    mean = jnp.sum(states, axis=0, keepdims=True) * (1.0 / members)
    anomaly = states - mean
    pull = target - precision * mean
    left = split3(anomaly * precision)
    right = split3(anomaly)
    gram = dot_nt(left[0], right[0]) + (
        (dot_nt(left[0], right[1]) + dot_nt(left[1], right[0]))
        + (dot_nt(left[0], right[2]) + dot_nt(left[2], right[0]) + dot_nt(left[1], right[1]))
    )
    diagonal = lax.broadcasted_iota(jnp.int32, gram.shape, 0) == lax.broadcasted_iota(jnp.int32, gram.shape, 1)
    gram = gram + jnp.where(diagonal, members - 1.0, 0.0)
    square = jnp.sum(jnp.sum(gram * gram, axis=0, keepdims=True), axis=1, keepdims=True)
    scale = jnp.sqrt(square)
    w_ref[...] = gram * (1.0 / scale)
    c_ref[...] = anomaly

    half = members // 2
    strips = (slice(0, half), slice(half, members))

    def newton(step, carry):
        w = split2(w_ref[...])
        s_ref[0], s_ref[1] = w
        p = [1.5 * w_ref[rows] - 0.5 * product((s_ref[0, rows], s_ref[1, rows]), w) for rows in strips]
        iter_c = c_ref[...]
        c = split2(iter_c)
        for rows in strips:
            c_ref[rows] = 1.5 * iter_c[rows] - 0.5 * product((s_ref[0, rows], s_ref[1, rows]), c)
        for rows, part in zip(strips, p):
            w_ref[rows] = 1.5 * part - 0.5 * product(split2(part), w)
        return carry

    lax.fori_loop(0, ITERS // 2, newton, 0)
    halfway()
    lax.fori_loop(ITERS // 2, ITERS - 1, newton, 0)
    iter_c = c_ref[...]
    final = 1.5 * iter_c - 0.5 * product(split2(w_ref[...]), split2(iter_c))
    inner = jnp.sum(final * pull, axis=1, keepdims=True)
    shift = jnp.sum(final * inner, axis=0, keepdims=True) * (1.0 / scale)
    coefficient = math.sqrt(members - 1.0) / jnp.sqrt(scale)
    return (mean + shift) + coefficient * final


ZERO, HEAD, TILE, LATE = 0, 1, 2, 3


def kernel(
    groups, tiles, bg_ref, diff_ref, adv_ref, where_ref, count_ref, value_ref, rinv_ref, out_ref,
    ext, sent, owned, result, obs, where, value, rinv, diff, adv, counts, w_ref, c_ref, s_ref,
    load_sem, halo_send, halo_recv, gather_send, gather_recv, back_send, back_recv, go_sem, first_sem, tile_sem,
):
    me = lax.axis_index("mem")
    tile = lax.axis_index("tile")
    cols, local, entries = sent.shape
    chunks = cols // groups
    members = groups * local
    right, left = lax.rem(tile + 1, tiles), lax.rem(tile + tiles - 1, tiles)

    loads = [
        pltpu.make_async_copy(bg_ref.at[index], ext.at[pl.ds(2, cols), index], load_sem.at[index])
        for index in range(local)
    ]
    small = ((diff_ref, diff), (adv_ref, adv), (count_ref, counts), (where_ref, where), (value_ref, value), (rinv_ref, rinv))
    loads += [
        pltpu.make_async_copy(source, target, load_sem.at[local + index]) for index, (source, target) in enumerate(small)
    ]
    barrier = pltpu.get_barrier_semaphore()

    strip, side = lax.div(me, 8), lax.rem(lax.div(me, 4), 2)
    lows = [lax.rem(me + index, 4) for index in range(4)]

    def peers(action):
        def visit(step, carry):
            action(lax.rem(me + step, groups))
            return carry

        def block(base, begin, index):
            first = base + 8 * lax.rem(strip + index, 4)
            for low in lows[begin:]:
                action(first + low)

        def far(index, carry):
            block(4 * (1 - side), 0, index)
            return carry

        def near(index, carry):
            block(4 * side, 0, index)
            return carry

        if groups != 32:
            lax.fori_loop(1, groups, visit, 0)
        else:
            lax.fori_loop(0, 4, far, 0)
            block(4 * side, 1, 0)
            lax.fori_loop(1, 4, near, 0)

    def tell(semaphore, peer, **where_to):
        pl.semaphore_signal(semaphore, inc=1, device_id={"mem": peer, **where_to}, device_id_type=MESH)

    @pl.when(me == ZERO)
    def _():
        tell(barrier, LATE)

    @pl.when(me != ZERO)
    def _():
        peers(lambda peer: pl.when((peer == HEAD) | (peer > LATE))(lambda: tell(barrier, peer)))

    for load in loads:
        load.start()

    @pl.when((me == HEAD) | (me > LATE))
    def _():
        pl.semaphore_wait(barrier, groups - 2)

    @pl.when(me == HEAD)
    def _():
        tell(go_sem, TILE)
        tell(go_sem, LATE)

    @pl.when((me == TILE) | (me == LATE))
    def _():
        pl.semaphore_wait(go_sem, 1)

    @pl.when(me == ZERO)
    def _():
        pl.semaphore_wait(first_sem, 1)

    for load in loads[:local + 2]:
        load.wait()
    diffusion = diff[...]
    advection = adv[...]

    def forecast(begin, end):
        width = min(8, groups)
        for start in range(begin, end, width):
            stop = min(start + width, end)
            cells = ext[start:stop + 4]
            half = advance(cells[:-2], cells[1:-1], cells[2:], diffusion, advection)
            sent[start:stop] = advance(half[:-2], half[1:-1], half[2:], diffusion, advection)

    mine = pl.ds(pl.multiple_of(me * local, local), local)

    def hand_over(chunk, peer):
        pltpu.make_async_remote_copy(
            src_ref=sent.at[chunk * groups + peer], dst_ref=owned.at[chunk, mine],
            send_sem=gather_send.at[chunk], recv_sem=gather_recv.at[chunk],
            device_id={"mem": peer}, device_id_type=MESH).start()

    def keep(chunk):
        owned[chunk, mine, :] = sent[chunk * groups + me]

    last = chunks - 1
    forecast(groups, 2 * groups)
    keep(1)
    peers(lambda peer: pl.when(peer != ZERO)(lambda: hand_over(1, peer)))

    @pl.when(me == LATE)
    def _():
        pl.semaphore_wait(barrier, 1)
        peers(lambda peer: tell(first_sem, peer))
        tell(barrier, TILE, tile=left)
        tell(barrier, TILE, tile=right)

    @pl.when((me != LATE) & (me != ZERO))
    def _():
        pl.semaphore_wait(first_sem, 1)

    @pl.when(me != ZERO)
    def _():
        hand_over(1, ZERO)

    for chunk in range(2, last):
        forecast(chunk * groups, (chunk + 1) * groups)
        keep(chunk)
        peers(lambda peer: hand_over(chunk, peer))
    forecast(last * groups, cols - 2)
    forecast(2, groups)

    tail = pltpu.make_async_remote_copy(
        src_ref=ext.at[pl.ds(cols, 2)], dst_ref=ext.at[pl.ds(0, 2)], send_sem=halo_send.at[0], recv_sem=halo_recv.at[0],
        device_id={"tile": right}, device_id_type=MESH)
    head = pltpu.make_async_remote_copy(
        src_ref=ext.at[pl.ds(2, 2)], dst_ref=ext.at[pl.ds(cols + 2, 2)], send_sem=halo_send.at[1], recv_sem=halo_recv.at[1],
        device_id={"tile": left}, device_id_type=MESH)

    def announce():
        @pl.when(me == TILE)
        def _():
            pl.semaphore_wait(barrier, 2)
            peers(lambda peer: tell(tile_sem, peer))

    def exchange_edges():
        @pl.when(me != TILE)
        def _():
            pl.semaphore_wait(tile_sem, 1)

        tail.start()
        head.start()

    @pl.when(tile != 0)
    def _():
        announce()
        exchange_edges()

    peers(lambda peer: pl.when(peer < groups - 2)(lambda: hand_over(last, peer)))
    peers(lambda peer: pl.when(peer > 1)(lambda: hand_over(0, peer)))


    for load in loads[local + 2:]:
        load.wait()
    for chunk in range(chunks):
        row = pl.ds(chunk * groups + me, 1)
        lanes = lax.broadcasted_iota(jnp.int32, counts.shape, 1)
        count = jnp.sum(jnp.where(lanes == chunk * groups + me, counts[...], 0), axis=1, keepdims=True)
        obs[chunk] = observe(where[row, :], count, value[row, :], rinv[row, :], entries)

    def send_edges():
        tail.wait()
        head.wait()
        forecast(0, 2)
        forecast(cols - 2, cols)
        keep(0)
        keep(last)
        for chunk, owner in ((last, groups - 2), (last, groups - 1), (0, 0), (0, 1)):
            pl.when(me != owner)(functools.partial(hand_over, chunk, owner))

    bulk = (groups - 1) * local

    def column(step, carry):
        chunk = lax.rem(step + 1, chunks)
        chunk = jnp.where((me >= groups // 2) & (step >= last - 1), (step - (last - 1)) * last, chunk)
        pltpu.make_async_remote_copy(
            src_ref=owned.at[chunk, pl.ds(0, bulk)], dst_ref=owned.at[chunk, pl.ds(0, bulk)],
            send_sem=gather_send.at[chunk], recv_sem=gather_recv.at[chunk],
            device_id={"mem": me}, device_id_type=MESH).wait_recv()
        pl.when((step == 0) & (tile == 0))(announce)

        def halfway():
            pl.when((step == 0) & (tile == 0))(exchange_edges)
            pl.when(step == 1)(send_edges)

        result[chunk] = analyse(owned[chunk], obs[chunk], w_ref, c_ref, s_ref, members, halfway)
        at = chunk * groups + me
        peers(lambda peer: pltpu.make_async_remote_copy(
            src_ref=result.at[chunk, pl.ds(pl.multiple_of(peer * local, local), local)], dst_ref=out_ref.at[at],
            send_sem=back_send.at[chunk], recv_sem=back_recv.at[chunk],
            device_id={"mem": peer}, device_id_type=MESH).start())
        out_ref[at] = result[chunk, mine, :]
        return carry

    lax.fori_loop(0, chunks, column, 0)
    for chunk in range(chunks):
        pltpu.make_async_remote_copy(
            src_ref=owned.at[chunk, pl.ds(0, bulk)], dst_ref=owned.at[chunk, pl.ds(0, bulk)],
            send_sem=gather_send.at[chunk], recv_sem=gather_recv.at[chunk],
            device_id={"mem": me}, device_id_type=MESH).wait_send()
        pltpu.make_async_remote_copy(
            src_ref=out_ref.at[pl.ds(0, groups - 1)], dst_ref=out_ref.at[pl.ds(0, groups - 1)],
            send_sem=back_send.at[chunk], recv_sem=back_recv.at[chunk],
            device_id={"mem": me}, device_id_type=MESH).wait()


def body(groups, tiles, background, diffusion, advection, obs_where, obs_count, obs_value, obs_rinv):
    local, cols, entries = background.shape
    chunks = cols // groups
    members = local * groups
    vmem = pl.BlockSpec(memory_space=pltpu.VMEM)
    hbm = pl.BlockSpec(memory_space=pltpu.HBM)
    slots = obs_where.shape[2]
    result = pl.pallas_call(
        functools.partial(kernel, groups, tiles),
        out_shape=pltpu.VMEM((cols, local, entries), F32),
        in_specs=[hbm] * 7,
        out_specs=vmem,
        scratch_shapes=[
            pltpu.VMEM((cols + 4, local, entries), F32),
            pltpu.VMEM((cols, local, entries), F32),
            pltpu.VMEM((chunks, members, entries), F32),
            pltpu.VMEM((chunks, members, entries), F32),
            pltpu.VMEM((chunks, 8, entries), F32),
            pltpu.VMEM((cols, slots), jnp.int32),
            pltpu.VMEM((cols, slots), F32),
            pltpu.VMEM((cols, slots), F32),
            pltpu.VMEM((1, entries), F32),
            pltpu.VMEM((1, entries), F32),
            pltpu.VMEM((1, cols), jnp.int32),
            pltpu.VMEM((members, members), F32),
            pltpu.VMEM((members, entries), F32),
            pltpu.VMEM((2, members, members), BF16),
            pltpu.SemaphoreType.DMA((local + 6,)),
            pltpu.SemaphoreType.DMA((2,)),
            pltpu.SemaphoreType.DMA((2,)),
            pltpu.SemaphoreType.DMA((chunks,)),
            pltpu.SemaphoreType.DMA((chunks,)),
            pltpu.SemaphoreType.DMA((chunks,)),
            pltpu.SemaphoreType.DMA((chunks,)),
            pltpu.SemaphoreType.REGULAR,
            pltpu.SemaphoreType.REGULAR,
            pltpu.SemaphoreType.REGULAR,
        ],
        compiler_params=pltpu.CompilerParams(collective_id=0, has_side_effects=True, vmem_limit_bytes=48 << 20),
    )(*(
        pltpu.with_memory_space_constraint(operand, pltpu.HBM)
        for operand in (
            background, diffusion[None, :], advection[None, :], obs_where[0], obs_count, obs_value[0], obs_rinv[0],
        )
    ))
    return jnp.transpose(result, (1, 0, 2))


def solution(mesh):
    return jax.shard_map(
        functools.partial(body, mesh.shape["mem"], mesh.shape["tile"]),
        mesh=mesh,
        in_specs=(
            P("mem", "tile", None),
            P(),
            P(),
            P("tile", None, None),
            P("tile", None),
            P("tile", None, None),
            P("tile", None, None),
        ),
        out_specs=P("mem", "tile", None),
        check_vma=False,
    )
```

```python
import functools
import math

import jax
import jax.numpy as jnp
from jax import lax
from jax.experimental import pallas as pl
from jax.experimental.pallas import tpu as pltpu
from jax.sharding import PartitionSpec as P

ITERS = 12
F32 = jnp.float32
BF16 = jnp.bfloat16
MESH = pl.DeviceIdType.MESH


def split2(a):
    high = a.astype(BF16)
    return high, (a - high.astype(F32)).astype(BF16)


def split3(a):
    high = a.astype(BF16)
    rest = a - high.astype(F32)
    middle = rest.astype(BF16)
    return high, middle, (rest - middle.astype(F32)).astype(BF16)


def dot(a, b):
    return jnp.dot(a, b, preferred_element_type=F32)


def dot_nt(a, b):
    return lax.dot_general(a, b, (((1,), (1,)), ((), ())), preferred_element_type=F32)


def product(a, b):
    return dot(a[0], b[0]) + (dot(a[0], b[1]) + dot(a[1], b[0]))


def advance(left, middle, right, diffusion, advection):
    return middle + diffusion * (left - 2.0 * middle + right) + advection * (0.5 * (left - right))


def observe(where, count, value, rinv, entries):
    slots = where.shape[1]
    mask = (lax.broadcasted_iota(jnp.int32, (1, slots), 1) < count).astype(F32)
    weight = rinv * mask
    terms = split3(weight) + split3(weight * value)
    row = lax.broadcasted_iota(jnp.int32, (8, slots), 0)
    stacked = jnp.zeros((8, slots), F32)
    for index, term in enumerate(terms):
        stacked = jnp.where(row == index, term.astype(F32), stacked)
    onehot = (lax.broadcasted_iota(jnp.int32, (entries, slots), 0) == where).astype(F32)
    return dot_nt(stacked.astype(BF16), onehot.astype(BF16))


def analyse(states, obs, w_ref, c_ref, s_ref, members, halfway):
    precision = obs[0:1] + (obs[1:2] + obs[2:3])
    target = obs[3:4] + (obs[4:5] + obs[5:6])
    mean = jnp.sum(states, axis=0, keepdims=True) * (1.0 / members)
    anomaly = states - mean
    pull = target - precision * mean
    left = split3(anomaly * precision)
    right = split3(anomaly)
    gram = dot_nt(left[0], right[0]) + (
        (dot_nt(left[0], right[1]) + dot_nt(left[1], right[0]))
        + (dot_nt(left[0], right[2]) + dot_nt(left[2], right[0]) + dot_nt(left[1], right[1]))
    )
    diagonal = lax.broadcasted_iota(jnp.int32, gram.shape, 0) == lax.broadcasted_iota(jnp.int32, gram.shape, 1)
    gram = gram + jnp.where(diagonal, members - 1.0, 0.0)
    square = jnp.sum(jnp.sum(gram * gram, axis=0, keepdims=True), axis=1, keepdims=True)
    scale = jnp.sqrt(square)
    w_ref[...] = gram * (1.0 / scale)
    c_ref[...] = anomaly

    half = members // 2
    strips = (slice(0, half), slice(half, members))

    def newton(step, carry):
        w = split2(w_ref[...])
        s_ref[0], s_ref[1] = w
        p = [1.5 * w_ref[rows] - 0.5 * product((s_ref[0, rows], s_ref[1, rows]), w) for rows in strips]
        iter_c = c_ref[...]
        c = split2(iter_c)
        for rows in strips:
            c_ref[rows] = 1.5 * iter_c[rows] - 0.5 * product((s_ref[0, rows], s_ref[1, rows]), c)
        for rows, part in zip(strips, p):
            w_ref[rows] = 1.5 * part - 0.5 * product(split2(part), w)
        return carry

    lax.fori_loop(0, ITERS // 2, newton, 0)
    halfway()
    lax.fori_loop(ITERS // 2, ITERS - 1, newton, 0)
    iter_c = c_ref[...]
    final = 1.5 * iter_c - 0.5 * product(split2(w_ref[...]), split2(iter_c))
    inner = jnp.sum(final * pull, axis=1, keepdims=True)
    shift = jnp.sum(final * inner, axis=0, keepdims=True) * (1.0 / scale)
    coefficient = math.sqrt(members - 1.0) / jnp.sqrt(scale)
    return (mean + shift) + coefficient * final


ZERO, HEAD, TILE, LATE = 0, 1, 2, 3


def kernel(
    groups, tiles, bg_ref, diff_ref, adv_ref, where_ref, count_ref, value_ref, rinv_ref, out_ref,
    ext, sent, owned, result, obs, where, value, rinv, diff, adv, counts, w_ref, c_ref, s_ref,
    load_sem, halo_send, halo_recv, gather_send, gather_recv, back_send, back_recv, go_sem, first_sem, tile_sem,
):
    me = lax.axis_index("mem")
    tile = lax.axis_index("tile")
    cols, local, entries = sent.shape
    chunks = cols // groups
    members = groups * local
    right, left = lax.rem(tile + 1, tiles), lax.rem(tile + tiles - 1, tiles)

    loads = [
        pltpu.make_async_copy(bg_ref.at[index], ext.at[pl.ds(2, cols), index], load_sem.at[index])
        for index in range(local)
    ]
    small = ((diff_ref, diff), (adv_ref, adv), (count_ref, counts), (where_ref, where), (value_ref, value), (rinv_ref, rinv))
    loads += [
        pltpu.make_async_copy(source, target, load_sem.at[local + index]) for index, (source, target) in enumerate(small)
    ]
    barrier = pltpu.get_barrier_semaphore()

    strip, side = lax.div(me, 8), lax.rem(lax.div(me, 4), 2)
    lows = [lax.rem(me + index, 4) for index in range(4)]

    def peers(action, same=True, others=True):
        def visit(step, carry):
            action(lax.rem(me + step, groups))
            return carry

        def block(base, begin, index):
            first = base + 8 * lax.rem(strip + index, 4)
            for low in lows[begin:]:
                action(first + low)

        def far(index, carry):
            block(4 * (1 - side), 0, index)
            return carry

        def near(index, carry):
            block(4 * side, 0, index)
            return carry

        if groups != 32:
            if others:
                lax.fori_loop(1, groups, visit, 0)
        else:
            if others:
                lax.fori_loop(1, 4, far, 0)
            if same:
                block(4 * (1 - side), 0, 0)
                block(4 * side, 1, 0)
            if others:
                lax.fori_loop(1, 4, near, 0)

    def tell(semaphore, peer, **where_to):
        pl.semaphore_signal(semaphore, inc=1, device_id={"mem": peer, **where_to}, device_id_type=MESH)

    @pl.when(me == ZERO)
    def _():
        tell(barrier, LATE)

    @pl.when(me != ZERO)
    def _():
        peers(lambda peer: pl.when((peer == HEAD) | (peer > LATE))(lambda: tell(barrier, peer)))

    for load in loads:
        load.start()

    @pl.when((me == HEAD) | (me > LATE))
    def _():
        pl.semaphore_wait(barrier, groups - 2)

    @pl.when(me == HEAD)
    def _():
        tell(go_sem, TILE)
        tell(go_sem, LATE)

    @pl.when((me == TILE) | (me == LATE))
    def _():
        pl.semaphore_wait(go_sem, 1)

    @pl.when(me == ZERO)
    def _():
        pl.semaphore_wait(first_sem, 1)

    for load in loads[:local + 2]:
        load.wait()
    diffusion = diff[...]
    advection = adv[...]

    def forecast(begin, end):
        width = min(8, groups)
        for start in range(begin, end, width):
            stop = min(start + width, end)
            cells = ext[start:stop + 4]
            half = advance(cells[:-2], cells[1:-1], cells[2:], diffusion, advection)
            sent[start:stop] = advance(half[:-2], half[1:-1], half[2:], diffusion, advection)

    mine = pl.ds(pl.multiple_of(me * local, local), local)

    def hand_over(chunk, peer):
        pltpu.make_async_remote_copy(
            src_ref=sent.at[chunk * groups + peer], dst_ref=owned.at[chunk, mine],
            send_sem=gather_send.at[chunk], recv_sem=gather_recv.at[chunk],
            device_id={"mem": peer}, device_id_type=MESH).start()

    def keep(chunk):
        owned[chunk, mine, :] = sent[chunk * groups + me]

    last = chunks - 1
    forecast(groups, 2 * groups)
    keep(1)
    peers(lambda peer: pl.when(peer != ZERO)(lambda: hand_over(1, peer)))

    @pl.when(me == LATE)
    def _():
        pl.semaphore_wait(barrier, 1)
        peers(lambda peer: tell(first_sem, peer))
        tell(barrier, TILE, tile=left)
        tell(barrier, TILE, tile=right)

    @pl.when((me != LATE) & (me != ZERO))
    def _():
        pl.semaphore_wait(first_sem, 1)

    @pl.when(me != ZERO)
    def _():
        hand_over(1, ZERO)

    for chunk in range(2, last):
        forecast(chunk * groups, (chunk + 1) * groups)
        keep(chunk)
        peers(lambda peer: hand_over(chunk, peer))
    forecast(last * groups, cols - 2)
    forecast(2, groups)

    tail = pltpu.make_async_remote_copy(
        src_ref=ext.at[pl.ds(cols, 2)], dst_ref=ext.at[pl.ds(0, 2)], send_sem=halo_send.at[0], recv_sem=halo_recv.at[0],
        device_id={"tile": right}, device_id_type=MESH)
    head = pltpu.make_async_remote_copy(
        src_ref=ext.at[pl.ds(2, 2)], dst_ref=ext.at[pl.ds(cols + 2, 2)], send_sem=halo_send.at[1], recv_sem=halo_recv.at[1],
        device_id={"tile": left}, device_id_type=MESH)

    def announce():
        @pl.when(me == TILE)
        def _():
            pl.semaphore_wait(barrier, 2)
            peers(lambda peer: tell(tile_sem, peer))

    def exchange_edges():
        @pl.when(me != TILE)
        def _():
            pl.semaphore_wait(tile_sem, 1)

        tail.start()
        head.start()

    @pl.when(tile != 0)
    def _():
        announce()
        exchange_edges()

    to_last = lambda peer: pl.when(peer < groups - 2)(lambda: hand_over(last, peer))
    to_first = lambda peer: pl.when(peer > 1)(lambda: hand_over(0, peer))
    peers(to_last, same=False)
    peers(to_first, same=False)

    def send_same():
        peers(to_last, others=False)
        peers(to_first, others=False)

    for load in loads[local + 2:]:
        load.wait()
    for chunk in range(chunks):
        row = pl.ds(chunk * groups + me, 1)
        lanes = lax.broadcasted_iota(jnp.int32, counts.shape, 1)
        count = jnp.sum(jnp.where(lanes == chunk * groups + me, counts[...], 0), axis=1, keepdims=True)
        obs[chunk] = observe(where[row, :], count, value[row, :], rinv[row, :], entries)

    def send_edges():
        tail.wait()
        head.wait()
        forecast(0, 2)
        forecast(cols - 2, cols)
        keep(0)
        keep(last)
        for chunk, owner in ((last, groups - 2), (last, groups - 1), (0, 0), (0, 1)):
            pl.when(me != owner)(functools.partial(hand_over, chunk, owner))

    bulk = (groups - 1) * local

    def column(step, carry):
        chunk = lax.rem(step + 1, chunks)
        chunk = jnp.where((me >= groups // 2) & (step >= last - 1), (step - (last - 1)) * last, chunk)
        pltpu.make_async_remote_copy(
            src_ref=owned.at[chunk, pl.ds(0, bulk)], dst_ref=owned.at[chunk, pl.ds(0, bulk)],
            send_sem=gather_send.at[chunk], recv_sem=gather_recv.at[chunk],
            device_id={"mem": me}, device_id_type=MESH).wait_recv()
        pl.when(step == 0)(send_same)
        pl.when((step == 0) & (tile == 0))(announce)

        def halfway():
            pl.when((step == 0) & (tile == 0))(exchange_edges)
            pl.when(step == 1)(send_edges)

        result[chunk] = analyse(owned[chunk], obs[chunk], w_ref, c_ref, s_ref, members, halfway)
        at = chunk * groups + me
        peers(lambda peer: pltpu.make_async_remote_copy(
            src_ref=result.at[chunk, pl.ds(pl.multiple_of(peer * local, local), local)], dst_ref=out_ref.at[at],
            send_sem=back_send.at[chunk], recv_sem=back_recv.at[chunk],
            device_id={"mem": peer}, device_id_type=MESH).start())
        out_ref[at] = result[chunk, mine, :]
        return carry

    lax.fori_loop(0, chunks, column, 0)
    for chunk in range(chunks):
        pltpu.make_async_remote_copy(
            src_ref=owned.at[chunk, pl.ds(0, bulk)], dst_ref=owned.at[chunk, pl.ds(0, bulk)],
            send_sem=gather_send.at[chunk], recv_sem=gather_recv.at[chunk],
            device_id={"mem": me}, device_id_type=MESH).wait_send()
        pltpu.make_async_remote_copy(
            src_ref=out_ref.at[pl.ds(0, groups - 1)], dst_ref=out_ref.at[pl.ds(0, groups - 1)],
            send_sem=back_send.at[chunk], recv_sem=back_recv.at[chunk],
            device_id={"mem": me}, device_id_type=MESH).wait()


def body(groups, tiles, background, diffusion, advection, obs_where, obs_count, obs_value, obs_rinv):
    local, cols, entries = background.shape
    chunks = cols // groups
    members = local * groups
    vmem = pl.BlockSpec(memory_space=pltpu.VMEM)
    hbm = pl.BlockSpec(memory_space=pltpu.HBM)
    slots = obs_where.shape[2]
    result = pl.pallas_call(
        functools.partial(kernel, groups, tiles),
        out_shape=pltpu.VMEM((cols, local, entries), F32),
        in_specs=[hbm] * 7,
        out_specs=vmem,
        scratch_shapes=[
            pltpu.VMEM((cols + 4, local, entries), F32),
            pltpu.VMEM((cols, local, entries), F32),
            pltpu.VMEM((chunks, members, entries), F32),
            pltpu.VMEM((chunks, members, entries), F32),
            pltpu.VMEM((chunks, 8, entries), F32),
            pltpu.VMEM((cols, slots), jnp.int32),
            pltpu.VMEM((cols, slots), F32),
            pltpu.VMEM((cols, slots), F32),
            pltpu.VMEM((1, entries), F32),
            pltpu.VMEM((1, entries), F32),
            pltpu.VMEM((1, cols), jnp.int32),
            pltpu.VMEM((members, members), F32),
            pltpu.VMEM((members, entries), F32),
            pltpu.VMEM((2, members, members), BF16),
            pltpu.SemaphoreType.DMA((local + 6,)),
            pltpu.SemaphoreType.DMA((2,)),
            pltpu.SemaphoreType.DMA((2,)),
            pltpu.SemaphoreType.DMA((chunks,)),
            pltpu.SemaphoreType.DMA((chunks,)),
            pltpu.SemaphoreType.DMA((chunks,)),
            pltpu.SemaphoreType.DMA((chunks,)),
            pltpu.SemaphoreType.REGULAR,
            pltpu.SemaphoreType.REGULAR,
            pltpu.SemaphoreType.REGULAR,
        ],
        compiler_params=pltpu.CompilerParams(collective_id=0, has_side_effects=True, vmem_limit_bytes=48 << 20),
    )(*(
        pltpu.with_memory_space_constraint(operand, pltpu.HBM)
        for operand in (
            background, diffusion[None, :], advection[None, :], obs_where[0], obs_count, obs_value[0], obs_rinv[0],
        )
    ))
    return jnp.transpose(result, (1, 0, 2))


def solution(mesh):
    return jax.shard_map(
        functools.partial(body, mesh.shape["mem"], mesh.shape["tile"]),
        mesh=mesh,
        in_specs=(
            P("mem", "tile", None),
            P(),
            P(),
            P("tile", None, None),
            P("tile", None),
            P("tile", None, None),
            P("tile", None, None),
        ),
        out_specs=P("mem", "tile", None),
        check_vma=False,
    )
```

```python
import functools
import math

import jax
import jax.numpy as jnp
from jax import lax
from jax.experimental import pallas as pl
from jax.experimental.pallas import tpu as pltpu
from jax.sharding import PartitionSpec as P

ITERS = 12
F32 = jnp.float32
BF16 = jnp.bfloat16
MESH = pl.DeviceIdType.MESH


def split2(a):
    high = a.astype(BF16)
    return high, (a - high.astype(F32)).astype(BF16)


def split3(a):
    high = a.astype(BF16)
    rest = a - high.astype(F32)
    middle = rest.astype(BF16)
    return high, middle, (rest - middle.astype(F32)).astype(BF16)


def dot(a, b):
    return jnp.dot(a, b, preferred_element_type=F32)


def dot_nt(a, b):
    return lax.dot_general(a, b, (((1,), (1,)), ((), ())), preferred_element_type=F32)


def product(a, b):
    return dot(a[0], b[0]) + (dot(a[0], b[1]) + dot(a[1], b[0]))


def advance(left, middle, right, diffusion, advection):
    return middle + diffusion * (left - 2.0 * middle + right) + advection * (0.5 * (left - right))


def observe(where, count, value, rinv, entries):
    slots = where.shape[1]
    mask = (lax.broadcasted_iota(jnp.int32, (1, slots), 1) < count).astype(F32)
    weight = rinv * mask
    terms = split3(weight) + split3(weight * value)
    row = lax.broadcasted_iota(jnp.int32, (8, slots), 0)
    stacked = jnp.zeros((8, slots), F32)
    for index, term in enumerate(terms):
        stacked = jnp.where(row == index, term.astype(F32), stacked)
    onehot = (lax.broadcasted_iota(jnp.int32, (entries, slots), 0) == where).astype(F32)
    return dot_nt(stacked.astype(BF16), onehot.astype(BF16))


def analyse(states, obs, w_ref, c_ref, s_ref, members, halfway):
    precision = obs[0:1] + (obs[1:2] + obs[2:3])
    target = obs[3:4] + (obs[4:5] + obs[5:6])
    mean = jnp.sum(states, axis=0, keepdims=True) * (1.0 / members)
    anomaly = states - mean
    pull = target - precision * mean
    left = split3(anomaly * precision)
    right = split3(anomaly)
    gram = dot_nt(left[0], right[0]) + (
        (dot_nt(left[0], right[1]) + dot_nt(left[1], right[0]))
        + (dot_nt(left[0], right[2]) + dot_nt(left[2], right[0]) + dot_nt(left[1], right[1]))
    )
    diagonal = lax.broadcasted_iota(jnp.int32, gram.shape, 0) == lax.broadcasted_iota(jnp.int32, gram.shape, 1)
    gram = gram + jnp.where(diagonal, members - 1.0, 0.0)
    square = jnp.sum(jnp.sum(gram * gram, axis=0, keepdims=True), axis=1, keepdims=True)
    scale = jnp.sqrt(square)
    w_ref[...] = gram * (1.0 / scale)
    c_ref[...] = anomaly

    half = members // 2
    strips = (slice(0, half), slice(half, members))

    def newton(step, carry):
        w = split2(w_ref[...])
        s_ref[0], s_ref[1] = w
        p = [1.5 * w_ref[rows] - 0.5 * product((s_ref[0, rows], s_ref[1, rows]), w) for rows in strips]
        iter_c = c_ref[...]
        c = split2(iter_c)
        for rows in strips:
            c_ref[rows] = 1.5 * iter_c[rows] - 0.5 * product((s_ref[0, rows], s_ref[1, rows]), c)
        for rows, part in zip(strips, p):
            w_ref[rows] = 1.5 * part - 0.5 * product(split2(part), w)
        return carry

    lax.fori_loop(0, ITERS // 2, newton, 0)
    halfway()
    lax.fori_loop(ITERS // 2, ITERS - 1, newton, 0)
    iter_c = c_ref[...]
    final = 1.5 * iter_c - 0.5 * product(split2(w_ref[...]), split2(iter_c))
    inner = jnp.sum(final * pull, axis=1, keepdims=True)
    shift = jnp.sum(final * inner, axis=0, keepdims=True) * (1.0 / scale)
    coefficient = math.sqrt(members - 1.0) / jnp.sqrt(scale)
    return (mean + shift) + coefficient * final


ZERO, HEAD, TILE, LATE = 0, 1, 2, 3


def kernel(
    groups, tiles, bg_ref, diff_ref, adv_ref, where_ref, count_ref, value_ref, rinv_ref, out_ref,
    ext, sent, owned, result, obs, where, value, rinv, diff, adv, counts, w_ref, c_ref, s_ref,
    load_sem, halo_send, halo_recv, gather_send, gather_recv, back_send, back_recv, go_sem, first_sem, tile_sem,
):
    me = lax.axis_index("mem")
    tile = lax.axis_index("tile")
    cols, local, entries = sent.shape
    chunks = cols // groups
    members = groups * local
    right, left = lax.rem(tile + 1, tiles), lax.rem(tile + tiles - 1, tiles)

    loads = [
        pltpu.make_async_copy(bg_ref.at[index], ext.at[pl.ds(2, cols), index], load_sem.at[index])
        for index in range(local)
    ]
    small = ((diff_ref, diff), (adv_ref, adv), (count_ref, counts), (where_ref, where), (value_ref, value), (rinv_ref, rinv))
    loads += [
        pltpu.make_async_copy(source, target, load_sem.at[local + index]) for index, (source, target) in enumerate(small)
    ]
    barrier = pltpu.get_barrier_semaphore()

    strip, side = lax.div(me, 8), lax.rem(lax.div(me, 4), 2)
    lows = [lax.rem(me + index, 4) for index in range(4)]

    def peers(action, same=True, others=True):
        def visit(step, carry):
            action(lax.rem(me + step, groups))
            return carry

        def block(base, begin, index):
            first = base + 8 * lax.rem(strip + index, 4)
            for low in lows[begin:]:
                action(first + low)

        def far(index, carry):
            block(4 * (1 - side), 0, index)
            return carry

        def near(index, carry):
            block(4 * side, 0, index)
            return carry

        if groups != 32:
            if others:
                lax.fori_loop(1, groups, visit, 0)
        else:
            if others:
                lax.fori_loop(1, 4, far, 0)
                lax.fori_loop(1, 4, near, 0)
            if same:
                block(4 * (1 - side), 0, 0)
                block(4 * side, 1, 0)

    def tell(semaphore, peer, **where_to):
        pl.semaphore_signal(semaphore, inc=1, device_id={"mem": peer, **where_to}, device_id_type=MESH)

    @pl.when(me == ZERO)
    def _():
        tell(barrier, LATE)

    @pl.when(me != ZERO)
    def _():
        peers(lambda peer: pl.when((peer == HEAD) | (peer > LATE))(lambda: tell(barrier, peer)))

    for load in loads:
        load.start()

    @pl.when((me == HEAD) | (me > LATE))
    def _():
        pl.semaphore_wait(barrier, groups - 2)

    @pl.when(me == HEAD)
    def _():
        tell(go_sem, TILE)
        tell(go_sem, LATE)

    @pl.when((me == TILE) | (me == LATE))
    def _():
        pl.semaphore_wait(go_sem, 1)

    @pl.when(me == ZERO)
    def _():
        pl.semaphore_wait(first_sem, 1)

    for load in loads[:local + 2]:
        load.wait()
    diffusion = diff[...]
    advection = adv[...]

    def forecast(begin, end):
        width = min(8, groups)
        for start in range(begin, end, width):
            stop = min(start + width, end)
            cells = ext[start:stop + 4]
            half = advance(cells[:-2], cells[1:-1], cells[2:], diffusion, advection)
            sent[start:stop] = advance(half[:-2], half[1:-1], half[2:], diffusion, advection)

    mine = pl.ds(pl.multiple_of(me * local, local), local)

    def hand_over(chunk, peer):
        pltpu.make_async_remote_copy(
            src_ref=sent.at[chunk * groups + peer], dst_ref=owned.at[chunk, mine],
            send_sem=gather_send.at[chunk], recv_sem=gather_recv.at[chunk],
            device_id={"mem": peer}, device_id_type=MESH).start()

    def keep(chunk):
        owned[chunk, mine, :] = sent[chunk * groups + me]

    last = chunks - 1
    forecast(groups, 2 * groups)
    keep(1)
    peers(lambda peer: pl.when(peer != ZERO)(lambda: hand_over(1, peer)))

    @pl.when(me == LATE)
    def _():
        pl.semaphore_wait(barrier, 1)
        peers(lambda peer: tell(first_sem, peer))
        tell(barrier, TILE, tile=left)
        tell(barrier, TILE, tile=right)

    @pl.when((me != LATE) & (me != ZERO))
    def _():
        pl.semaphore_wait(first_sem, 1)

    @pl.when(me != ZERO)
    def _():
        hand_over(1, ZERO)

    for chunk in range(2, last):
        forecast(chunk * groups, (chunk + 1) * groups)
        keep(chunk)
        peers(lambda peer: hand_over(chunk, peer))
    forecast(last * groups, cols - 2)
    forecast(2, groups)

    tail = pltpu.make_async_remote_copy(
        src_ref=ext.at[pl.ds(cols, 2)], dst_ref=ext.at[pl.ds(0, 2)], send_sem=halo_send.at[0], recv_sem=halo_recv.at[0],
        device_id={"tile": right}, device_id_type=MESH)
    head = pltpu.make_async_remote_copy(
        src_ref=ext.at[pl.ds(2, 2)], dst_ref=ext.at[pl.ds(cols + 2, 2)], send_sem=halo_send.at[1], recv_sem=halo_recv.at[1],
        device_id={"tile": left}, device_id_type=MESH)

    def announce():
        @pl.when(me == TILE)
        def _():
            pl.semaphore_wait(barrier, 2)
            peers(lambda peer: tell(tile_sem, peer))

    def exchange_edges():
        @pl.when(me != TILE)
        def _():
            pl.semaphore_wait(tile_sem, 1)

        tail.start()
        head.start()

    @pl.when(tile != 0)
    def _():
        announce()
        exchange_edges()

    to_last = lambda peer: pl.when(peer < groups - 2)(lambda: hand_over(last, peer))
    to_first = lambda peer: pl.when(peer > 1)(lambda: hand_over(0, peer))
    peers(to_last, same=False)
    peers(to_first, same=False)

    def send_same():
        peers(to_last, others=False)
        peers(to_first, others=False)

    for load in loads[local + 2:]:
        load.wait()
    for chunk in range(chunks):
        row = pl.ds(chunk * groups + me, 1)
        lanes = lax.broadcasted_iota(jnp.int32, counts.shape, 1)
        count = jnp.sum(jnp.where(lanes == chunk * groups + me, counts[...], 0), axis=1, keepdims=True)
        obs[chunk] = observe(where[row, :], count, value[row, :], rinv[row, :], entries)

    def send_edges():
        tail.wait()
        head.wait()
        forecast(0, 2)
        forecast(cols - 2, cols)
        keep(0)
        keep(last)
        for chunk, owner in ((last, groups - 2), (last, groups - 1), (0, 0), (0, 1)):
            pl.when(me != owner)(functools.partial(hand_over, chunk, owner))

    bulk = (groups - 1) * local

    def column(step, carry):
        chunk = lax.rem(step + 1, chunks)
        chunk = jnp.where((me >= groups // 2) & (step >= last - 1), (step - (last - 1)) * last, chunk)
        pltpu.make_async_remote_copy(
            src_ref=owned.at[chunk, pl.ds(0, bulk)], dst_ref=owned.at[chunk, pl.ds(0, bulk)],
            send_sem=gather_send.at[chunk], recv_sem=gather_recv.at[chunk],
            device_id={"mem": me}, device_id_type=MESH).wait_recv()
        pl.when(step == 0)(send_same)
        pl.when((step == 0) & (tile == 0))(announce)

        def halfway():
            pl.when((step == 0) & (tile == 0))(exchange_edges)
            pl.when(step == 1)(send_edges)

        result[chunk] = analyse(owned[chunk], obs[chunk], w_ref, c_ref, s_ref, members, halfway)
        at = chunk * groups + me
        peers(lambda peer: pltpu.make_async_remote_copy(
            src_ref=result.at[chunk, pl.ds(pl.multiple_of(peer * local, local), local)], dst_ref=out_ref.at[at],
            send_sem=back_send.at[chunk], recv_sem=back_recv.at[chunk],
            device_id={"mem": peer}, device_id_type=MESH).start())
        out_ref[at] = result[chunk, mine, :]
        return carry

    lax.fori_loop(0, chunks, column, 0)
    for chunk in range(chunks):
        pltpu.make_async_remote_copy(
            src_ref=owned.at[chunk, pl.ds(0, bulk)], dst_ref=owned.at[chunk, pl.ds(0, bulk)],
            send_sem=gather_send.at[chunk], recv_sem=gather_recv.at[chunk],
            device_id={"mem": me}, device_id_type=MESH).wait_send()
        pltpu.make_async_remote_copy(
            src_ref=out_ref.at[pl.ds(0, groups - 1)], dst_ref=out_ref.at[pl.ds(0, groups - 1)],
            send_sem=back_send.at[chunk], recv_sem=back_recv.at[chunk],
            device_id={"mem": me}, device_id_type=MESH).wait()


def body(groups, tiles, background, diffusion, advection, obs_where, obs_count, obs_value, obs_rinv):
    local, cols, entries = background.shape
    chunks = cols // groups
    members = local * groups
    vmem = pl.BlockSpec(memory_space=pltpu.VMEM)
    hbm = pl.BlockSpec(memory_space=pltpu.HBM)
    slots = obs_where.shape[2]
    result = pl.pallas_call(
        functools.partial(kernel, groups, tiles),
        out_shape=pltpu.VMEM((cols, local, entries), F32),
        in_specs=[hbm] * 7,
        out_specs=vmem,
        scratch_shapes=[
            pltpu.VMEM((cols + 4, local, entries), F32),
            pltpu.VMEM((cols, local, entries), F32),
            pltpu.VMEM((chunks, members, entries), F32),
            pltpu.VMEM((chunks, members, entries), F32),
            pltpu.VMEM((chunks, 8, entries), F32),
            pltpu.VMEM((cols, slots), jnp.int32),
            pltpu.VMEM((cols, slots), F32),
            pltpu.VMEM((cols, slots), F32),
            pltpu.VMEM((1, entries), F32),
            pltpu.VMEM((1, entries), F32),
            pltpu.VMEM((1, cols), jnp.int32),
            pltpu.VMEM((members, members), F32),
            pltpu.VMEM((members, entries), F32),
            pltpu.VMEM((2, members, members), BF16),
            pltpu.SemaphoreType.DMA((local + 6,)),
            pltpu.SemaphoreType.DMA((2,)),
            pltpu.SemaphoreType.DMA((2,)),
            pltpu.SemaphoreType.DMA((chunks,)),
            pltpu.SemaphoreType.DMA((chunks,)),
            pltpu.SemaphoreType.DMA((chunks,)),
            pltpu.SemaphoreType.DMA((chunks,)),
            pltpu.SemaphoreType.REGULAR,
            pltpu.SemaphoreType.REGULAR,
            pltpu.SemaphoreType.REGULAR,
        ],
        compiler_params=pltpu.CompilerParams(collective_id=0, has_side_effects=True, vmem_limit_bytes=48 << 20),
    )(*(
        pltpu.with_memory_space_constraint(operand, pltpu.HBM)
        for operand in (
            background, diffusion[None, :], advection[None, :], obs_where[0], obs_count, obs_value[0], obs_rinv[0],
        )
    ))
    return jnp.transpose(result, (1, 0, 2))


def solution(mesh):
    return jax.shard_map(
        functools.partial(body, mesh.shape["mem"], mesh.shape["tile"]),
        mesh=mesh,
        in_specs=(
            P("mem", "tile", None),
            P(),
            P(),
            P("tile", None, None),
            P("tile", None),
            P("tile", None, None),
            P("tile", None, None),
        ),
        out_specs=P("mem", "tile", None),
        check_vma=False,
    )
```
